256 devices in a mesh: rows: 8 (over y, x_hi), weeks: 32 (over z, x_lo, core).
Axes of the slice: x: 4 (x_hi: 2, x_lo: 2; x = x_hi * 2 + x_lo), y: 4, z: 8, core: 2. Of those that a mesh axis runs over, the one named last changes fastest.
Arguments:
- counts: int32 [32768, 4096], P('rows', 'weeks'), may hold values from 0 to 15
- offsets: bfloat16 [32768, 4096], P('rows', 'weeks'), may hold values from -1.2 to 2.52
- loadings: float32 [32768, 64], P('rows'), may hold values from -0.4 to 0.4
- factors: float32 [4096, 64], P('weeks'), may hold values from -0.4 to 0.4
Outputs:
- new_loadings: float32 [32768, 64], P('rows')
- new_factors: float32 [4096, 64], P('weeks')
The draws below stay inside these ranges and needn't reach their ends.
All inputs are finite; a program needn't handle non-finite values.
Results may differ from the reference program's by a relative error of at most 0.0003.
Values sent between devices are 32-bit elements; how exact they have to be, the bound alone decides.
A program may use at most 64 MiB of HBM per device.

```python
import jax
import jax.numpy as jnp
from jax import lax

K = 64
ITERS = 2
ROWS = 32768
WEEKS = 4096


def level_pair(key):
    row_level = jax.random.randint(jax.random.fold_in(key, 101), (ROWS,), 1, 9, dtype=jnp.int32)
    week_level = jax.random.randint(jax.random.fold_in(key, 102), (WEEKS,), 1, 9, dtype=jnp.int32)
    return (row_level, week_level)


def draw_counts(key, part):
    row_level, week_level = level_pair(key)
    ceiling = row_level[:, None] + week_level[None, :]
    return jax.random.randint(jax.random.fold_in(key, 103), (ROWS, WEEKS), 0, ceiling, dtype=jnp.int32)


def draw_offsets(key, part):
    row_level, week_level = level_pair(key)
    mean_count = (row_level[:, None] + week_level[None, :] - 1).astype(jnp.float32) * 0.5
    jitter_key = jax.random.fold_in(key, 104)
    jitter = 0.25 * jnp.clip(jax.random.normal(jitter_key, (ROWS, WEEKS), jnp.float32), -2.0, 2.0)
    return (jnp.log(mean_count) + jitter).astype(jnp.bfloat16)


def scaled_entries(key, count_rows, level):
    entries = jnp.clip(jax.random.normal(key, (count_rows, K), jnp.float32), -3.0, 3.0)
    row_scale = 0.1 * jnp.sqrt(level.astype(jnp.float32) / 4.5)
    return entries * row_scale[:, None]


def draw_loadings(key, part):
    row_level, week_level = level_pair(key)
    return scaled_entries(jax.random.fold_in(key, 105), ROWS, row_level)


def draw_factors(key, part):
    row_level, week_level = level_pair(key)
    return scaled_entries(jax.random.fold_in(key, 106), WEEKS, week_level)


def setup_inputs(seed: int = 0) -> dict:
    streams_of = jax.random.split(jax.random.key(seed), 5)
    return {
        "counts": draw_counts(jax.random.fold_in(streams_of[4], 71), 0),
        "offsets": draw_offsets(jax.random.fold_in(streams_of[4], 71), 0),
        "loadings": draw_loadings(jax.random.fold_in(streams_of[4], 71), 0),
        "factors": draw_factors(jax.random.fold_in(streams_of[4], 71), 0),
    }


HIGH = lax.Precision.HIGHEST


def reference(counts, offsets, loadings, factors):
    counts_f = counts.astype(jnp.float32)
    offsets_f = offsets.astype(jnp.float32)
    load = loadings
    fac = factors
    for step in range(ITERS):
        eta = offsets_f + jnp.dot(load, fac.T, precision=HIGH)
        mu_val = jnp.exp(eta)
        resid = counts_f - mu_val
        grad_a = jnp.dot(resid, fac, precision=HIGH)
        curv_a = jnp.dot(mu_val, fac * fac, precision=HIGH)
        load = load + grad_a / (1.0 + curv_a)
        eta = offsets_f + jnp.dot(load, fac.T, precision=HIGH)
        mu_val = jnp.exp(eta)
        resid = counts_f - mu_val
        grad_b = jnp.dot(resid.T, load, precision=HIGH)
        curv_b = jnp.dot(mu_val.T, load * load, precision=HIGH)
        fac = fac + grad_b / (1.0 + curv_b)
    return load, fac
```

```python
import functools

import jax
import jax.numpy as jnp
from jax import lax
from jax.experimental import pallas as pl
from jax.experimental.pallas import tpu as pltpu
from jax.sharding import PartitionSpec as P

ITERS = 2
F32 = jnp.float32
BF16 = jnp.bfloat16
MESH = pl.DeviceIdType.MESH
NZ = 8
R = 8


def far_first(j):
    return 4 + (1 - 2 * lax.rem(j, 2)) * lax.div(j + 1, 2)


def split(v):
    hi = v.astype(BF16)
    lo = (v - hi.astype(F32)).astype(BF16)
    return hi, lo


def mm(a, b):
    return jnp.dot(a, b, preferred_element_type=F32)


def kernel(
    counts, offs, load, fac, at_out, fac_out,
    cnt, obf, off, osend, a0, xmat, weta, w1, w3, g1, g2,
    bt, at1, at2, xs, xr, so, zs, zr, gs, gr,
    s_loc, s_cnt, s_off, s_bt, s_send, s_x, s_z, s_agz, s_agx, s_g, s_b, s_sib, s_out,
):
    r = lax.axis_index("rows")
    w = lax.axis_index("weeks")
    z = lax.div(w, 4)
    xl = lax.rem(lax.div(w, 2), 2)
    c = lax.rem(w, 2)
    sib = (r, w + 1 - 2 * c)
    xp = (r, w + 2 - 4 * xl)
    own = xl * 8 + z

    def zdev(o):
        return (r, lax.rem(w + 4 * o, 32))

    def rdev(idx):
        return (lax.rem(idx, 8), w - c + lax.div(idx, 8))

    def zsrc(j):
        return lax.rem(z + 8 - far_first(j), 8)

    def remote(src, dst, ss, rs, dev):
        return pltpu.make_async_remote_copy(
            src_ref=src, dst_ref=dst, send_sem=ss, recv_sem=rs, device_id=dev, device_id_type=MESH
        )

    def wait_bytes(ref, sem):
        pltpu.make_async_copy(ref, ref, sem).wait()

    me = c * 8 + r
    barrier = pltpu.get_barrier_semaphore()

    def greet_z(j, carry):
        pl.semaphore_signal(barrier, inc=1, device_id=zdev(j), device_id_type=MESH)
        return carry

    def greet_r(t, carry):
        pl.semaphore_signal(barrier, inc=1, device_id=rdev(lax.rem(me + t, 16)), device_id_type=MESH)
        return carry

    ld_off = pltpu.make_async_copy(offs, obf, s_loc.at[0])
    ld_cnt = pltpu.make_async_copy(counts.at[c], cnt.at[c], s_loc.at[1])
    ld_a0 = pltpu.make_async_copy(load.at[c], a0, s_loc.at[2])
    ld_off.start()
    ld_a0.start()
    ld_cnt.start()
    lax.fori_loop(1, 8, greet_z, 0)
    lax.fori_loop(1, 16, greet_r, 0)
    pl.semaphore_signal(barrier, inc=1, device_id=xp, device_id_type=MESH)

    bt[0, c] = fac[...].T.reshape(8, 8, 128)
    ld_off.wait()
    pl.semaphore_wait(barrier, 23)

    remote(bt.at[0, c], bt.at[0, c], s_send.at[0], s_bt, sib).start()

    def swap(j, carry):
        d = lax.rem(z + far_first(j), 8)
        remote(counts.at[1 - c, :, d], cnt.at[c, :, d], s_send.at[1], s_cnt.at[j], sib).start()
        for x in range(2):
            osend[x, d] = obf[1 - c, x, d].astype(F32)
        remote(osend.at[:, d], off.at[c, :, d], s_send.at[2], s_off.at[j], sib).start()
        return carry

    lax.fori_loop(0, 8, swap, 0)

    def prepare(d, carry):
        for x in range(2):
            off[c, x, d] = obf[c, x, d].astype(F32)
        return carry

    lax.fori_loop(0, 8, prepare, 0)
    ld_a0.wait()

    def first_x(b, carry):
        hi, lo = split(a0[b])
        xmat[b] = jnp.concatenate([hi.astype(F32), lo.astype(F32)], axis=1).astype(BF16)
        return carry

    lax.fori_loop(0, 16, first_x, 0)
    ld_cnt.wait()

    def week_weights(it):
        b = jnp.concatenate([bt[it, 0].reshape(64, 128), bt[it, 1].reshape(64, 128)], axis=1)
        bh, bl = split(b)
        qh, ql = split(b * b)
        weta[...] = jnp.concatenate([bh, bh, bl, bl], axis=0)
        bh, bl, qh, ql = (v.astype(F32) for v in (bh, bl, qh, ql))
        w1[...] = jnp.concatenate([bh, -qh, bl, -ql], axis=0).T.astype(BF16)
        zero = jnp.zeros_like(qh)
        w3[...] = jnp.concatenate([zero, qh, zero, ql], axis=0).T.astype(BF16)

    def residual(x, d):
        xb = xmat[x * 8 + d]
        eta = mm(jnp.concatenate([xb, xb], axis=1), weta[...])
        o = jnp.concatenate([off[0, x, d], off[1, x, d]], axis=1)
        n = jnp.concatenate([cnt[0, x, d], cnt[1, x, d]], axis=1).astype(F32)
        res = n - jnp.exp(eta + o)
        rh, rl = split(res)
        return rh, rl, n.astype(BF16)

    def left(x, d):
        rh, rl, n = residual(x, d)
        o = mm(rh, w1[...]) + mm(n, w3[...])
        return o[:, :128] + o[:, 128:] + mm(rl, w1[:, :128])

    def right(at, x, d):
        a = at[x * 8 + d]
        hi, lo = split(a)
        ph, pw = split(a * a)
        xmat[x * 8 + d] = jnp.concatenate([hi.astype(F32), lo.astype(F32)], axis=0).T.astype(BF16)
        rh, rl, n = residual(x, d)
        lt = jnp.concatenate([hi, -ph, lo, -pw], axis=0)
        g1[...] += mm(lt, rh)
        g2[:128] += mm(lt[:128], rl)
        g2[128:] += mm(jnp.concatenate([ph, pw], axis=0), n)

    for it in range(ITERS):
        last = it == ITERS - 1
        at = at2.at[c] if last else at1
        if it == 0:
            pltpu.make_async_copy(bt.at[0, 1 - c], bt.at[0, 1 - c], s_bt).wait()
        week_weights(it)

        def a_step(j, carry, it=it):
            @pl.when(j < 8)
            def _():
                d = lax.rem(z + far_first(j), 8)
                if it == 0:
                    wait_bytes(cnt.at[1 - c, :, d], s_cnt.at[j])
                    wait_bytes(off.at[1 - c, :, d], s_off.at[j])
                xs[it, j] = left(1 - xl, d)
                remote(xs.at[it, j], xr.at[it, j], s_send.at[3], s_x.at[it, j], xp).start()
                so[j] = left(xl, d)

            @pl.when(j >= 3)
            def _():
                k = j - 3
                wait_bytes(xr.at[it, k], s_x.at[it, k])
                zs[it, k] = so[k] + xr[it, k]

                @pl.when(k < 7)
                def _():
                    remote(
                        zs.at[it, k], zr.at[it, k], s_send.at[4], s_z.at[it, k], zdev(far_first(k))
                    ).start()

            return carry

        lax.fori_loop(0, 11, a_step, 0)

        def z_sum(k, total, it=it):
            wait_bytes(zr.at[it, k], s_z.at[it, k])
            return total + zr[it, k]

        total = lax.fori_loop(0, 7, z_sum, zs[it, 7]).T
        old = a0[own].T if it == 0 else at1[own]
        at[own] = old + total[:64] / (1.0 + total[64:])

        remote(at.at[own], at.at[own], s_send.at[5], s_agx.at[it, 7], xp).start()

        def ag_send(j, carry, it=it, at=at):
            remote(at.at[own], at.at[own], s_send.at[6], s_agz.at[it, j], zdev(far_first(j))).start()
            return carry

        lax.fori_loop(0, 7, ag_send, 0)

        g1[...] = jnp.zeros_like(g1)
        g2[...] = jnp.zeros_like(g2)
        right(at, xl, z)

        def b_step(k, carry, it=it, at=at):
            @pl.when(k < 7)
            def _():
                d = zsrc(k)
                blk = at.at[xl * 8 + d]
                wait_bytes(blk, s_agz.at[it, k])
                remote(blk, blk, s_send.at[5], s_agx.at[it, k], xp).start()
                right(at, xl, d)

            @pl.when(k >= 2)
            def _():
                k2 = lax.rem(k + 5, 8)
                d = zsrc(k2)
                wait_bytes(at.at[(1 - xl) * 8 + d], s_agx.at[it, k2])
                right(at, 1 - xl, d)

            return carry

        lax.fori_loop(0, 10, b_step, 0)

        if last:
            remote(at2.at[c], at2.at[c], s_send.at[7], s_sib, sib).start()
            pltpu.make_async_copy(at2.at[c], at_out.at[c], s_out.at[0]).start()

        grad = g1[0:64] + g1[128:192] + g2[0:64]
        curv = g1[64:128] + g1[192:256] + g2[64:128] + g2[128:192] + g2[192:256]
        for h in range(2):
            for o in range(8):
                gs[it, h * 8 + o, 0] = grad[8 * o : 8 * o + 8, 128 * h : 128 * h + 128]
                gs[it, h * 8 + o, 1] = curv[8 * o : 8 * o + 8, 128 * h : 128 * h + 128]

        def g_send(t, carry, it=it):
            idx = lax.rem(me + t, 16)
            remote(gs.at[it, idx], gr.at[it, t - 1], s_send.at[8], s_g.at[it], rdev(idx)).start()
            return carry

        lax.fori_loop(1, 16, g_send, 0)
        wait_bytes(gr.at[it], s_g.at[it])
        tot = gs[it, me]
        for t in range(15):
            tot = tot + gr[it, t]
        bt[it + 1, c, r] = bt[it, c, r] + tot[0] / (1.0 + tot[1])
        mine = bt.at[it + 1, c, r]

        if last:
            def b_send(t, carry, mine=mine, it=it):
                dev = (lax.rem(r + t, 8), w)
                remote(mine, mine, s_send.at[9], s_b.at[it], dev).start()
                return carry

            lax.fori_loop(1, 8, b_send, 0)
            wait_bytes(gr.at[it, pl.ds(0, 7), 0], s_b.at[it])
        else:
            def b_send(t, carry, mine=mine, it=it):
                remote(mine, mine, s_send.at[9], s_b.at[it], rdev(lax.rem(me + t, 16))).start()
                return carry

            lax.fori_loop(1, 16, b_send, 0)
            wait_bytes(gr.at[it, :, 0], s_b.at[it])

    fac_out[...] = bt[ITERS, c].reshape(64, 128).T
    wait_bytes(at2.at[1 - c], s_sib)
    pltpu.make_async_copy(at2.at[1 - c], at_out.at[1 - c], s_out.at[1]).start()

    wait_bytes(bt.at[0, c], s_send.at[0])
    wait_bytes(cnt.at[c], s_send.at[1])
    wait_bytes(osend, s_send.at[2])
    wait_bytes(xs, s_send.at[3])
    wait_bytes(zs.at[:, pl.ds(0, 7)], s_send.at[4])
    wait_bytes(at1, s_send.at[5])
    wait_bytes(at1.at[pl.ds(0, 14)], s_send.at[6])
    wait_bytes(at2.at[c], s_send.at[7])
    wait_bytes(gr, s_send.at[8])
    wait_bytes(gr.at[0, :, 0], s_send.at[9])
    wait_bytes(gr.at[0, pl.ds(0, 7), 0], s_send.at[9])
    pltpu.make_async_copy(at2.at[c], at_out.at[c], s_out.at[0]).wait()
    pltpu.make_async_copy(at2.at[1 - c], at_out.at[1 - c], s_out.at[1]).wait()


def local(counts, offsets, loadings, factors):
    any_spec = pl.BlockSpec(memory_space=pl.ANY)
    vmem_spec = pl.BlockSpec(memory_space=pltpu.VMEM)
    dma = pltpu.SemaphoreType.DMA
    at_out, fac_out = pl.pallas_call(
        kernel,
        out_shape=(
            jax.ShapeDtypeStruct((2, 16, 64, 128), F32),
            jax.ShapeDtypeStruct((128, 64), F32),
        ),
        in_specs=[any_spec, any_spec, any_spec, vmem_spec],
        out_specs=(any_spec, vmem_spec),
        scratch_shapes=[
            pltpu.VMEM((2, 2, 8, 128, 128), jnp.int32),
            pltpu.VMEM((2, 2, 8, 128, 128), BF16),
            pltpu.VMEM((2, 2, 8, 128, 128), F32),
            pltpu.VMEM((2, 8, 128, 128), F32),
            pltpu.VMEM((16, 128, 64), F32),
            pltpu.VMEM((16, 128, 128), BF16),
            pltpu.VMEM((256, 256), BF16),
            pltpu.VMEM((256, 256), BF16),
            pltpu.VMEM((256, 256), BF16),
            pltpu.VMEM((256, 256), F32),
            pltpu.VMEM((256, 256), F32),
            pltpu.VMEM((ITERS + 1, 2, 8, 8, 128), F32),
            pltpu.VMEM((16, 64, 128), F32),
            pltpu.VMEM((2, 16, 64, 128), F32),
            pltpu.VMEM((ITERS, 8, 128, 128), F32),
            pltpu.VMEM((ITERS, 8, 128, 128), F32),
            pltpu.VMEM((8, 128, 128), F32),
            pltpu.VMEM((ITERS, 8, 128, 128), F32),
            pltpu.VMEM((ITERS, 7, 128, 128), F32),
            pltpu.VMEM((ITERS, 16, 2, 8, 128), F32),
            pltpu.VMEM((ITERS, 15, 2, 8, 128), F32),
            dma((3,)),
            dma((8,)),
            dma((8,)),
            dma,
            dma((10,)),
            dma((ITERS, 8)),
            dma((ITERS, 7)),
            dma((ITERS, 7)),
            dma((ITERS, 8)),
            dma((ITERS,)),
            dma((ITERS,)),
            dma,
            dma((2,)),
        ],
        compiler_params=pltpu.CompilerParams(
            collective_id=0, has_side_effects=True, vmem_limit_bytes=48 * 1024 * 1024
        ),
        name="glm_pca",
    )(
        counts.reshape(2, 2, 8, 128, 128),
        offsets.reshape(2, 2, 8, 128, 128),
        loadings.reshape(2, 16, 128, 64),
        factors,
    )
    new_loadings = at_out.reshape(32, 64, 128).transpose(0, 2, 1).reshape(4096, 64)
    return new_loadings, fac_out


def solution(mesh):
    placed = (P("rows", "weeks"), P("rows", "weeks"), P("rows", None), P("weeks", None))
    return jax.shard_map(
        local,
        mesh=mesh,
        in_specs=placed,
        out_specs=(P("rows", None), P("weeks", None)),
        check_vma=False,
    )
```

```python
import functools

import jax
import jax.numpy as jnp
from jax import lax
from jax.experimental import pallas as pl
from jax.experimental.pallas import tpu as pltpu
from jax.sharding import PartitionSpec as P

ITERS = 2
F32 = jnp.float32
BF16 = jnp.bfloat16
MESH = pl.DeviceIdType.MESH
LATE = 3
LAG = 5
STAG = 1


def pack(digits):
    return sum(d * 8**i for i, d in enumerate(digits))


OWNERS = pack([4, 2, 6, 5, 3, 1, 7, 0])
TARGETS = pack([1, 1, 7, 5, 3, 1, 7])


def far_first(j):
    return 4 + (1 - 2 * lax.rem(j, 2)) * lax.div(j + 1, 2)


def split(v):
    hi = v.astype(BF16)
    lo = (v - hi.astype(F32)).astype(BF16)
    return hi, lo


def mm(a, b):
    return jnp.dot(a, b, preferred_element_type=F32)


def kernel(
    counts, offs, load, fac, at_out, fac_out,
    cnt, obf, off, osend, a0, xmat, weta, w1, w3, g1, g2,
    bt, at1, at2, xs, xr, so, zs, zr, gs, gr,
    s_loc, s_cnt, s_off, s_bt, s_send, s_x, s_z, s_agz, s_agx, s_g, s_b, s_sib, s_out,
):
    r = lax.axis_index("rows")
    w = lax.axis_index("weeks")
    z = lax.div(w, 4)
    xl = lax.rem(lax.div(w, 2), 2)
    c = lax.rem(w, 2)
    sib = (r, w + 1 - 2 * c)
    xp = (r, w + 2 - 4 * xl)
    own = xl * 8 + z

    def zdev(o):
        return (r, lax.rem(w + 4 * o, 32))

    def rdev(idx):
        return (lax.rem(idx, 8), w - c + lax.div(idx, 8))

    def zdst(seq):
        return lax.rem(z + lax.rem(seq, 8), 8)

    def zsrc(f):
        return lax.rem(z + 8 - far_first(f), 8)

    def remote(src, dst, ss, rs, dev):
        return pltpu.make_async_remote_copy(
            src_ref=src, dst_ref=dst, send_sem=ss, recv_sem=rs, device_id=dev, device_id_type=MESH
        )

    def wait_bytes(ref, sem):
        pltpu.make_async_copy(ref, ref, sem).wait()

    def put(h, b, carry):
        cols = pl.ds(pl.multiple_of((h * 16 + b) * 128, 128), 128)
        pltpu.make_async_copy(at2.at[h, b], at_out.at[:, cols], s_out).start()
        return carry

    me = c * 8 + r
    barrier = pltpu.get_barrier_semaphore()

    def greet_z(j, carry):
        pl.semaphore_signal(barrier, inc=1, device_id=zdev(j), device_id_type=MESH)
        return carry

    def greet_r(t, carry):
        pl.semaphore_signal(barrier, inc=1, device_id=rdev(lax.rem(me + t, 16)), device_id_type=MESH)
        return carry

    ld_off = pltpu.make_async_copy(offs, obf, s_loc.at[0])
    ld_cnt = pltpu.make_async_copy(counts.at[c], cnt.at[c], s_loc.at[1])
    ld_a0 = pltpu.make_async_copy(load.at[:, pl.ds(c * 2048, 2048)], a0, s_loc.at[2])
    ld_off.start()
    ld_a0.start()
    ld_cnt.start()
    lax.fori_loop(1, 8, greet_z, 0)
    lax.fori_loop(1, 16, greet_r, 0)
    pl.semaphore_signal(barrier, inc=1, device_id=xp, device_id_type=MESH)

    bt[0, c] = fac[...].reshape(8, 8, 128)

    def first(b):
        return a0[:, pl.ds(pl.multiple_of(b * 128, 128), 128)]

    def stack(hi, lo):
        return jnp.concatenate([hi.astype(F32), lo.astype(F32)], axis=0).T.astype(BF16)

    ld_off.wait()

    def widen(d, carry):
        for x in range(2):
            osend[x, d] = obf[1 - c, x, d].astype(F32)
            off[c, x, d] = obf[c, x, d].astype(F32)
        return carry

    lax.fori_loop(0, 8, widen, 0)
    ld_a0.wait()

    def first_x(b, carry):
        xmat[b] = stack(*split(first(b)))
        return carry

    lax.fori_loop(0, 16, first_x, 0)
    ld_cnt.wait()
    pl.semaphore_wait(barrier, 23)

    remote(bt.at[0, c], bt.at[0, c], s_send.at[0], s_bt, sib).start()

    def swap(k, seq):
        d = zdst(seq)
        remote(counts.at[1 - c, :, d], cnt.at[c, :, d], s_send.at[1], s_cnt.at[k], sib).start()
        remote(osend.at[:, d], off.at[c, :, d], s_send.at[2], s_off.at[k], sib).start()
        return lax.div(seq, 8)

    lax.fori_loop(0, 8, swap, OWNERS)

    def week_weights(it):
        b = jnp.concatenate([bt[it, 0].reshape(64, 128), bt[it, 1].reshape(64, 128)], axis=1)
        bh, bl = split(b)
        qh, ql = split(b * b)
        weta[...] = jnp.concatenate([bh, bh, bl, bl], axis=0)
        bh, bl, qh, ql = (v.astype(F32) for v in (bh, bl, qh, ql))
        w1[...] = jnp.concatenate([bh, -qh, bl, -ql], axis=0).T.astype(BF16)
        zero = jnp.zeros_like(qh)
        w3[...] = jnp.concatenate([zero, qh, zero, ql], axis=0).T.astype(BF16)

    def residual(x, d):
        xb = xmat[x * 8 + d]
        eta = mm(jnp.concatenate([xb, xb], axis=1), weta[...])
        o = jnp.concatenate([off[0, x, d], off[1, x, d]], axis=1)
        n = jnp.concatenate([cnt[0, x, d], cnt[1, x, d]], axis=1).astype(F32)
        res = n - jnp.exp(eta + o)
        rh, rl = split(res)
        return rh, rl, n.astype(BF16)

    def left(x, d):
        rh, rl, n = residual(x, d)
        o = mm(rh, w1[...]) + mm(n, w3[...])
        return o[:, :128] + o[:, 128:] + mm(rl, w1[:, :128])

    def right(at, x, d):
        a = at[x * 8 + d]
        hi, lo = split(a)
        ph, pw = split(a * a)
        xmat[x * 8 + d] = stack(hi, lo)
        rh, rl, n = residual(x, d)
        lt = jnp.concatenate([hi, -ph, lo, -pw], axis=0)
        g1[...] += mm(lt, rh)
        g2[:128] += mm(lt[:128], rl)
        g2[128:] += mm(jnp.concatenate([ph, pw], axis=0), n)

    for it in range(ITERS):
        last = it == ITERS - 1
        at = at2.at[c] if last else at1
        if it == 0:
            pltpu.make_async_copy(bt.at[0, 1 - c], bt.at[0, 1 - c], s_bt).wait()
        week_weights(it)

        def finish(it=it, at=at):
            def z_sum(f, total):
                wait_bytes(zr.at[it, f], s_z.at[it, f])
                return total + zr[it, f]

            total = lax.fori_loop(3, 7, z_sum, zs[it, 7]).T
            old = first(own) if it == 0 else at1[own]
            at[own] = old + total[:64] / (1.0 + total[64:])

            def ag_send(f, carry):
                remote(at.at[own], at.at[own], s_send.at[6], s_agz.at[it, f], zdev(far_first(f))).start()
                return carry

            lax.fori_loop(0, 7, ag_send, 0)
            remote(at.at[own], at.at[own], s_send.at[5], s_agx.at[it, 7], xp).start()

        def emit(j, d, x, it=it):
            v = left(x, d)

            @pl.when(x == xl)
            def _():
                so[j] = v

            @pl.when(x != xl)
            def _():
                xs[it, j] = v
                remote(xs.at[it, j], xr.at[it, j], s_send.at[3], s_x.at[it, j], xp).start()

        def a_one(j, seq, it=it, emit=emit):
            d = zdst(seq)
            if it == 0:
                wait_bytes(cnt.at[1 - c, :, d], s_cnt.at[j])
                wait_bytes(off.at[1 - c, :, d], s_off.at[j])
            emit(j, d, lax.rem(xl + 1 + c * STAG, 2))
            return lax.div(seq, 8)

        def a_two(j, carry, it=it, emit=emit):
            seq, target = carry

            @pl.when(j < 8)
            def _():
                emit(j, zdst(seq), lax.rem(xl + c * STAG, 2))

            f = j - LATE * c * STAG

            @pl.when((f >= 0) & (f < 8))
            def _():
                wait_bytes(xr.at[it, f], s_x.at[it, f])
                zs[it, f] = so[f] + xr[it, f]

                @pl.when((f >= 4) & (f < 7))
                def _():
                    wait_bytes(zr.at[it, f - 4], s_z.at[it, f - 4])
                    zs[it, f] += zr[it, f - 4]

                @pl.when(f < 7)
                def _():
                    remote(
                        zs.at[it, f], zr.at[it, f], s_send.at[4], s_z.at[it, f], zdev(lax.rem(target, 8))
                    ).start()

            return lax.div(seq, 8), lax.div(target, 8)

        lax.fori_loop(0, 8, a_one, OWNERS)
        delayed = TARGETS * (1 + c * STAG * (8**LATE - 1))
        lax.fori_loop(0, 8 + LATE * STAG, a_two, (jnp.int32(OWNERS), delayed))
        finish()

        g1[...] = jnp.zeros_like(g1)
        g2[...] = jnp.zeros_like(g2)

        def b_step(k, carry, it=it, at=at):
            @pl.when(k < 8)
            def _():
                f = k
                d = zsrc(f)

                @pl.when(f < 7)
                def _():
                    blk = at.at[xl * 8 + d]
                    wait_bytes(blk, s_agz.at[it, f])
                    remote(blk, blk, s_send.at[5], s_agx.at[it, f], xp).start()

                right(at, xl, d)

            @pl.when(k >= LAG)
            def _():
                f = k - LAG
                d = zsrc(f)
                wait_bytes(at.at[(1 - xl) * 8 + d], s_agx.at[it, f])
                right(at, 1 - xl, d)

            return carry

        lax.fori_loop(0, 8 + LAG, b_step, 0)

        if last:
            remote(at2.at[c], at2.at[c], s_send.at[7], s_sib, sib).start()
            lax.fori_loop(0, 16, functools.partial(put, c), 0)

        grad = g1[0:64] + g1[128:192] + g2[0:64]
        curv = g1[64:128] + g1[192:256] + g2[64:128] + g2[128:192] + g2[192:256]
        for h in range(2):
            for o in range(8):
                gs[it, h * 8 + o, 0] = grad[8 * o : 8 * o + 8, 128 * h : 128 * h + 128]
                gs[it, h * 8 + o, 1] = curv[8 * o : 8 * o + 8, 128 * h : 128 * h + 128]

        def g_send(t, carry, it=it):
            idx = lax.rem(me + t, 16)
            remote(gs.at[it, idx], gr.at[it, t - 1], s_send.at[8], s_g.at[it], rdev(idx)).start()
            return carry

        lax.fori_loop(1, 16, g_send, 0)
        wait_bytes(gr.at[it], s_g.at[it])
        tot = gs[it, me]
        for t in range(15):
            tot = tot + gr[it, t]
        bt[it + 1, c, r] = bt[it, c, r] + tot[0] / (1.0 + tot[1])
        mine = bt.at[it + 1, c, r]

        if last:
            def b_send(t, carry, mine=mine, it=it):
                dev = (lax.rem(r + t, 8), w)
                remote(mine, mine, s_send.at[9], s_b.at[it], dev).start()
                return carry

            lax.fori_loop(1, 8, b_send, 0)
            wait_bytes(gr.at[it, pl.ds(0, 7), 0], s_b.at[it])
        else:
            def b_send(t, carry, mine=mine, it=it):
                remote(mine, mine, s_send.at[9], s_b.at[it], rdev(lax.rem(me + t, 16))).start()
                return carry

            lax.fori_loop(1, 16, b_send, 0)
            wait_bytes(gr.at[it, :, 0], s_b.at[it])

    fac_out[...] = bt[ITERS, c].reshape(64, 128)
    wait_bytes(at2.at[1 - c], s_sib)
    lax.fori_loop(0, 16, functools.partial(put, 1 - c), 0)

    wait_bytes(bt.at[0, c], s_send.at[0])
    wait_bytes(cnt.at[c], s_send.at[1])
    wait_bytes(osend, s_send.at[2])
    wait_bytes(xs, s_send.at[3])
    wait_bytes(zs.at[:, pl.ds(0, 7)], s_send.at[4])
    wait_bytes(at1, s_send.at[5])
    wait_bytes(at1.at[pl.ds(0, 14)], s_send.at[6])
    wait_bytes(at2.at[c], s_send.at[7])
    wait_bytes(gr, s_send.at[8])
    wait_bytes(gr.at[0, :, 0], s_send.at[9])
    wait_bytes(gr.at[0, pl.ds(0, 7), 0], s_send.at[9])
    wait_bytes(at2, s_out)


def hand_over(a_ref, f_ref, a_out, f_out, a_buf, f_buf, sem_in, sem_out):
    parts = [(f_ref, f_buf, f_out)]
    for i in range(4):
        rows = pl.ds(16 * i, 16)
        parts.append((a_ref.at[rows], a_buf.at[rows], a_out.at[rows]))
    for i, (src, buf, _) in enumerate(parts):
        pltpu.make_async_copy(src, buf, sem_in.at[i]).start()
    for i, (src, buf, dst) in enumerate(parts):
        pltpu.make_async_copy(src, buf, sem_in.at[i]).wait()
        pltpu.make_async_copy(buf, dst, sem_out.at[i]).start()
    for i, (_, buf, dst) in enumerate(parts):
        pltpu.make_async_copy(buf, dst, sem_out.at[i]).wait()


def local(counts, offsets, loadings, factors):
    any_spec = pl.BlockSpec(memory_space=pl.ANY)
    hbm_spec = pl.BlockSpec(memory_space=pltpu.HBM)
    vmem_spec = pl.BlockSpec(memory_space=pltpu.VMEM)
    dma = pltpu.SemaphoreType.DMA
    at_out, fac_out = pl.pallas_call(
        kernel,
        out_shape=(
            jax.ShapeDtypeStruct((64, 4096), F32),
            jax.ShapeDtypeStruct((64, 128), F32),
        ),
        in_specs=[any_spec, any_spec, any_spec, vmem_spec],
        out_specs=(any_spec, vmem_spec),
        scratch_shapes=[
            pltpu.VMEM((2, 2, 8, 128, 128), jnp.int32),
            pltpu.VMEM((2, 2, 8, 128, 128), BF16),
            pltpu.VMEM((2, 2, 8, 128, 128), F32),
            pltpu.VMEM((2, 8, 128, 128), F32),
            pltpu.VMEM((64, 2048), F32),
            pltpu.VMEM((16, 128, 128), BF16),
            pltpu.VMEM((256, 256), BF16),
            pltpu.VMEM((256, 256), BF16),
            pltpu.VMEM((256, 256), BF16),
            pltpu.VMEM((256, 256), F32),
            pltpu.VMEM((256, 256), F32),
            pltpu.VMEM((ITERS + 1, 2, 8, 8, 128), F32),
            pltpu.VMEM((16, 64, 128), F32),
            pltpu.VMEM((2, 16, 64, 128), F32),
            pltpu.VMEM((ITERS, 8, 128, 128), F32),
            pltpu.VMEM((ITERS, 8, 128, 128), F32),
            pltpu.VMEM((8, 128, 128), F32),
            pltpu.VMEM((ITERS, 8, 128, 128), F32),
            pltpu.VMEM((ITERS, 7, 128, 128), F32),
            pltpu.VMEM((ITERS, 16, 2, 8, 128), F32),
            pltpu.VMEM((ITERS, 15, 2, 8, 128), F32),
            dma((3,)),
            dma((8,)),
            dma((8,)),
            dma,
            dma((10,)),
            dma((ITERS, 8)),
            dma((ITERS, 7)),
            dma((ITERS, 7)),
            dma((ITERS, 8)),
            dma((ITERS,)),
            dma((ITERS,)),
            dma,
            dma,
        ],
        compiler_params=pltpu.CompilerParams(
            collective_id=0, has_side_effects=True, vmem_limit_bytes=60 * 1024 * 1024
        ),
        name="glm_pca",
    )(
        counts.reshape(2, 2, 8, 128, 128),
        offsets.reshape(2, 2, 8, 128, 128),
        loadings.T,
        factors.T,
    )
    at_out, fac_out = pl.pallas_call(
        hand_over,
        out_shape=(
            jax.ShapeDtypeStruct((64, 4096), F32),
            jax.ShapeDtypeStruct((64, 128), F32),
        ),
        in_specs=[hbm_spec, hbm_spec],
        out_specs=(hbm_spec, hbm_spec),
        scratch_shapes=[pltpu.VMEM((64, 4096), F32), pltpu.VMEM((64, 128), F32), dma((5,)), dma((5,))],
        name="hand_over",
    )(at_out, fac_out)
    return at_out.T, fac_out.T


def solution(mesh):
    placed = (P("rows", "weeks"), P("rows", "weeks"), P("rows", None), P("weeks", None))
    return jax.shard_map(
        local,
        mesh=mesh,
        in_specs=placed,
        out_specs=(P("rows", None), P("weeks", None)),
        check_vma=False,
    )
```

```python
import functools

import jax
import jax.numpy as jnp
from jax import lax
from jax.experimental import pallas as pl
from jax.experimental.pallas import tpu as pltpu
from jax.sharding import PartitionSpec as P

ITERS = 2
F32 = jnp.float32
BF16 = jnp.bfloat16
MESH = pl.DeviceIdType.MESH
LATE = 3
LAG = 5
STAG = 1


def pack(digits):
    return sum(d * 8**i for i, d in enumerate(digits))


OWNERS = pack([4, 2, 6, 5, 3, 1, 7, 0])
TARGETS = pack([1, 1, 7, 5, 3, 1, 7])
OUTWARD = pack([0, 1, 7, 3, 5, 2, 6, 4])


def far_first(j):
    return 4 + (1 - 2 * lax.rem(j, 2)) * lax.div(j + 1, 2)


def split(v):
    hi = v.astype(BF16)
    lo = (v - hi.astype(F32)).astype(BF16)
    return hi, lo


def mm(a, b):
    return jnp.dot(a, b, preferred_element_type=F32)


def kernel(
    counts, offs, load, fac, at_out, fac_out,
    cnt, obf, off, osend, a0, xmat, weta, w1, w3, g1, g2,
    bt, at1, at2, xs, xr, so, zs, zr, gs, gr,
    s_loc, s_cnt, s_off, s_bt, s_send, s_x, s_z, s_agz, s_agx, s_g, s_b, s_sib, s_out,
):
    r = lax.axis_index("rows")
    w = lax.axis_index("weeks")
    z = lax.div(w, 4)
    xl = lax.rem(lax.div(w, 2), 2)
    c = lax.rem(w, 2)
    sib = (r, w + 1 - 2 * c)
    xp = (r, w + 2 - 4 * xl)
    own = xl * 8 + z

    def zdev(o):
        return (r, lax.rem(w + 4 * o, 32))

    def rdev(idx):
        return (lax.rem(idx, 8), w - c + lax.div(idx, 8))

    def zdst(seq):
        return lax.rem(z + lax.rem(seq, 8), 8)

    def zsrc(f):
        return lax.rem(z + 8 - far_first(f), 8)

    def remote(src, dst, ss, rs, dev):
        return pltpu.make_async_remote_copy(
            src_ref=src, dst_ref=dst, send_sem=ss, recv_sem=rs, device_id=dev, device_id_type=MESH
        )

    def wait_bytes(ref, sem):
        pltpu.make_async_copy(ref, ref, sem).wait()

    def put(h, b, carry):
        cols = pl.ds(pl.multiple_of((h * 16 + b) * 128, 128), 128)
        pltpu.make_async_copy(at2.at[h, b], at_out.at[:, cols], s_out).start()
        return carry

    me = c * 8 + r
    barrier = pltpu.get_barrier_semaphore()

    def greet_z(j, carry):
        pl.semaphore_signal(barrier, inc=1, device_id=zdev(j), device_id_type=MESH)
        return carry

    def greet_r(t, carry):
        pl.semaphore_signal(barrier, inc=1, device_id=rdev(lax.rem(me + t, 16)), device_id_type=MESH)
        return carry

    ld_off = pltpu.make_async_copy(offs, obf, s_loc.at[0])
    ld_cnt = pltpu.make_async_copy(counts.at[c], cnt.at[c], s_loc.at[1])
    ld_a0 = pltpu.make_async_copy(load.at[:, pl.ds(c * 2048, 2048)], a0, s_loc.at[2])
    ld_off.start()
    ld_a0.start()
    ld_cnt.start()
    lax.fori_loop(1, 8, greet_z, 0)
    lax.fori_loop(1, 16, greet_r, 0)
    pl.semaphore_signal(barrier, inc=1, device_id=xp, device_id_type=MESH)

    bt[0, c] = fac[...].reshape(8, 8, 128)

    def first(b):
        return a0[:, pl.ds(pl.multiple_of(b * 128, 128), 128)]

    def stack(hi, lo):
        return jnp.concatenate([hi.astype(F32), lo.astype(F32)], axis=0).T.astype(BF16)

    ld_off.wait()

    def widen(d, carry):
        for x in range(2):
            osend[x, d] = obf[1 - c, x, d].astype(F32)
            off[c, x, d] = obf[c, x, d].astype(F32)
        return carry

    lax.fori_loop(0, 8, widen, 0)
    ld_a0.wait()

    def first_x(b, carry):
        xmat[b] = stack(*split(first(b)))
        return carry

    lax.fori_loop(0, 16, first_x, 0)
    ld_cnt.wait()
    pl.semaphore_wait(barrier, 23)

    remote(bt.at[0, c], bt.at[0, c], s_send.at[0], s_bt, sib).start()

    def swap(k, seq):
        d = zdst(seq)
        remote(counts.at[1 - c, :, d], cnt.at[c, :, d], s_send.at[1], s_cnt.at[k], sib).start()
        remote(osend.at[:, d], off.at[c, :, d], s_send.at[2], s_off.at[k], sib).start()
        return lax.div(seq, 8)

    lax.fori_loop(0, 8, swap, OWNERS)

    def week_weights(it):
        b = jnp.concatenate([bt[it, 0].reshape(64, 128), bt[it, 1].reshape(64, 128)], axis=1)
        bh, bl = split(b)
        qh, ql = split(b * b)
        weta[...] = jnp.concatenate([bh, bh, bl, bl], axis=0)
        bh, bl, qh, ql = (v.astype(F32) for v in (bh, bl, qh, ql))
        w1[...] = jnp.concatenate([bh, -qh, bl, -ql], axis=0).T.astype(BF16)
        zero = jnp.zeros_like(qh)
        w3[...] = jnp.concatenate([zero, qh, zero, ql], axis=0).T.astype(BF16)

    def residual(x, d):
        xb = xmat[x * 8 + d]
        eta = mm(jnp.concatenate([xb, xb], axis=1), weta[...])
        o = jnp.concatenate([off[0, x, d], off[1, x, d]], axis=1)
        n = jnp.concatenate([cnt[0, x, d], cnt[1, x, d]], axis=1).astype(F32)
        res = n - jnp.exp(eta + o)
        rh, rl = split(res)
        return rh, rl, n.astype(BF16)

    def left(x, d):
        rh, rl, n = residual(x, d)
        o = mm(rh, w1[...]) + mm(n, w3[...])
        return o[:, :128] + o[:, 128:] + mm(rl, w1[:, :128])

    def right(at, x, d):
        a = at[x * 8 + d]
        hi, lo = split(a)
        ph, pw = split(a * a)
        xmat[x * 8 + d] = stack(hi, lo)
        rh, rl, n = residual(x, d)
        lt = jnp.concatenate([hi, -ph, lo, -pw], axis=0)
        g1[...] += mm(lt, rh)
        g2[:128] += mm(lt[:128], rl)
        g2[128:] += mm(jnp.concatenate([ph, pw], axis=0), n)

    for it in range(ITERS):
        last = it == ITERS - 1
        at = at2.at[c] if last else at1
        if it == 0:
            pltpu.make_async_copy(bt.at[0, 1 - c], bt.at[0, 1 - c], s_bt).wait()
        week_weights(it)

        def finish(it=it, at=at):
            def z_sum(f, total):
                wait_bytes(zr.at[it, f], s_z.at[it, f])
                return total + zr[it, f]

            total = lax.fori_loop(3, 7, z_sum, zs[it, 7]).T
            old = first(own) if it == 0 else at1[own]
            at[own] = old + total[:64] / (1.0 + total[64:])

            def ag_send(p, seq):
                remote(
                    at.at[own], at.at[own], s_send.at[6], s_agz.at[it, p], zdev(lax.rem(seq, 8))
                ).start()
                return lax.div(seq, 8)

            lax.fori_loop(0, 4, ag_send, OUTWARD // 8)
            remote(at.at[own], at.at[own], s_send.at[5], s_agx.at[it, 7], xp).start()

        def emit(j, d, x, it=it):
            v = left(x, d)

            @pl.when(x == xl)
            def _():
                so[j] = v

            @pl.when(x != xl)
            def _():
                xs[it, j] = v
                remote(xs.at[it, j], xr.at[it, j], s_send.at[3], s_x.at[it, j], xp).start()

        def a_one(j, seq, it=it, emit=emit):
            d = zdst(seq)
            if it == 0:
                wait_bytes(cnt.at[1 - c, :, d], s_cnt.at[j])
                wait_bytes(off.at[1 - c, :, d], s_off.at[j])
            emit(j, d, lax.rem(xl + 1 + c * STAG, 2))
            return lax.div(seq, 8)

        def a_two(j, carry, it=it, emit=emit):
            seq, target = carry

            @pl.when(j < 8)
            def _():
                emit(j, zdst(seq), lax.rem(xl + c * STAG, 2))

            f = j - LATE * c * STAG

            @pl.when((f >= 0) & (f < 8))
            def _():
                wait_bytes(xr.at[it, f], s_x.at[it, f])
                zs[it, f] = so[f] + xr[it, f]

                @pl.when((f >= 4) & (f < 7))
                def _():
                    wait_bytes(zr.at[it, f - 4], s_z.at[it, f - 4])
                    zs[it, f] += zr[it, f - 4]

                @pl.when(f < 7)
                def _():
                    remote(
                        zs.at[it, f], zr.at[it, f], s_send.at[4], s_z.at[it, f], zdev(lax.rem(target, 8))
                    ).start()

            return lax.div(seq, 8), lax.div(target, 8)

        lax.fori_loop(0, 8, a_one, OWNERS)
        delayed = TARGETS * (1 + c * STAG * (8**LATE - 1))
        lax.fori_loop(0, 8 + LATE * STAG, a_two, (jnp.int32(OWNERS), delayed))
        finish()

        g1[...] = jnp.zeros_like(g1)
        g2[...] = jnp.zeros_like(g2)

        def b_step(k, carry, it=it, at=at):
            seq, late = carry

            @pl.when(k < 8)
            def _():
                d = lax.rem(z + 8 - lax.rem(seq, 8), 8)

                @pl.when(k > 0)
                def _():
                    p = k - 1
                    blk = at.at[xl * 8 + d]
                    wait_bytes(blk, s_agz.at[it, p])

                    @pl.when(p < 3)
                    def _():
                        on = 1 + 6 * lax.rem(p, 2)
                        remote(blk, blk, s_send.at[6], s_agz.at[it, p + 4], zdev(on)).start()

                    remote(blk, blk, s_send.at[5], s_agx.at[it, p], xp).start()

                right(at, xl, d)

            @pl.when(k >= LAG)
            def _():
                d = lax.rem(z + 8 - lax.rem(late, 8), 8)
                wait_bytes(at.at[(1 - xl) * 8 + d], s_agx.at[it, lax.rem(k + 7 - LAG, 8)])
                right(at, 1 - xl, d)

            return lax.div(seq, 8), lax.select(k >= LAG, lax.div(late, 8), late)

        lax.fori_loop(0, 8 + LAG, b_step, (jnp.int32(OUTWARD), jnp.int32(OUTWARD)))

        if last:
            remote(at2.at[c], at2.at[c], s_send.at[7], s_sib, sib).start()
            lax.fori_loop(0, 16, functools.partial(put, c), 0)

        grad = g1[0:64] + g1[128:192] + g2[0:64]
        curv = g1[64:128] + g1[192:256] + g2[64:128] + g2[128:192] + g2[192:256]
        for h in range(2):
            for o in range(8):
                gs[it, h * 8 + o, 0] = grad[8 * o : 8 * o + 8, 128 * h : 128 * h + 128]
                gs[it, h * 8 + o, 1] = curv[8 * o : 8 * o + 8, 128 * h : 128 * h + 128]

        def g_send(t, carry, it=it):
            u = 1 + lax.rem(t + 3, 15)
            idx = lax.rem(me + u, 16)
            remote(gs.at[it, idx], gr.at[it, u - 1], s_send.at[8], s_g.at[it], rdev(idx)).start()
            return carry

        lax.fori_loop(1, 16, g_send, 0)
        wait_bytes(gr.at[it], s_g.at[it])
        tot = gs[it, me]
        for t in range(15):
            tot = tot + gr[it, t]
        bt[it + 1, c, r] = bt[it, c, r] + tot[0] / (1.0 + tot[1])
        mine = bt.at[it + 1, c, r]

        if last:
            def b_send(t, carry, mine=mine, it=it):
                dev = (lax.rem(r + t, 8), w)
                remote(mine, mine, s_send.at[9], s_b.at[it], dev).start()
                return carry

            lax.fori_loop(1, 8, b_send, 0)
            wait_bytes(gr.at[it, pl.ds(0, 7), 0], s_b.at[it])
        else:
            def b_send(t, carry, mine=mine, it=it):
                remote(mine, mine, s_send.at[9], s_b.at[it], rdev(lax.rem(me + 1 + lax.rem(t + 3, 15), 16))).start()
                return carry

            lax.fori_loop(1, 16, b_send, 0)
            wait_bytes(gr.at[it, :, 0], s_b.at[it])

    fac_out[...] = bt[ITERS, c].reshape(64, 128)
    wait_bytes(at2.at[1 - c], s_sib)
    lax.fori_loop(0, 16, functools.partial(put, 1 - c), 0)

    wait_bytes(bt.at[0, c], s_send.at[0])
    wait_bytes(cnt.at[c], s_send.at[1])
    wait_bytes(osend, s_send.at[2])
    wait_bytes(xs, s_send.at[3])
    wait_bytes(zs.at[:, pl.ds(0, 7)], s_send.at[4])
    wait_bytes(at1, s_send.at[5])
    wait_bytes(at1.at[pl.ds(0, 14)], s_send.at[6])
    wait_bytes(at2.at[c], s_send.at[7])
    wait_bytes(gr, s_send.at[8])
    wait_bytes(gr.at[0, :, 0], s_send.at[9])
    wait_bytes(gr.at[0, pl.ds(0, 7), 0], s_send.at[9])
    wait_bytes(at2, s_out)


def hand_over(a_ref, f_ref, a_out, f_out, a_buf, f_buf, sem_in, sem_out):
    parts = [(f_ref, f_buf, f_out)]
    for i in range(4):
        rows = pl.ds(16 * i, 16)
        parts.append((a_ref.at[rows], a_buf.at[rows], a_out.at[rows]))
    for i, (src, buf, _) in enumerate(parts):
        pltpu.make_async_copy(src, buf, sem_in.at[i]).start()
    for i, (src, buf, dst) in enumerate(parts):
        pltpu.make_async_copy(src, buf, sem_in.at[i]).wait()
        pltpu.make_async_copy(buf, dst, sem_out.at[i]).start()
    for i, (_, buf, dst) in enumerate(parts):
        pltpu.make_async_copy(buf, dst, sem_out.at[i]).wait()


def local(counts, offsets, loadings, factors):
    any_spec = pl.BlockSpec(memory_space=pl.ANY)
    hbm_spec = pl.BlockSpec(memory_space=pltpu.HBM)
    vmem_spec = pl.BlockSpec(memory_space=pltpu.VMEM)
    dma = pltpu.SemaphoreType.DMA
    at_out, fac_out = pl.pallas_call(
        kernel,
        out_shape=(
            jax.ShapeDtypeStruct((64, 4096), F32),
            jax.ShapeDtypeStruct((64, 128), F32),
        ),
        in_specs=[any_spec, any_spec, any_spec, vmem_spec],
        out_specs=(any_spec, vmem_spec),
        scratch_shapes=[
            pltpu.VMEM((2, 2, 8, 128, 128), jnp.int32),
            pltpu.VMEM((2, 2, 8, 128, 128), BF16),
            pltpu.VMEM((2, 2, 8, 128, 128), F32),
            pltpu.VMEM((2, 8, 128, 128), F32),
            pltpu.VMEM((64, 2048), F32),
            pltpu.VMEM((16, 128, 128), BF16),
            pltpu.VMEM((256, 256), BF16),
            pltpu.VMEM((256, 256), BF16),
            pltpu.VMEM((256, 256), BF16),
            pltpu.VMEM((256, 256), F32),
            pltpu.VMEM((256, 256), F32),
            pltpu.VMEM((ITERS + 1, 2, 8, 8, 128), F32),
            pltpu.VMEM((16, 64, 128), F32),
            pltpu.VMEM((2, 16, 64, 128), F32),
            pltpu.VMEM((ITERS, 8, 128, 128), F32),
            pltpu.VMEM((ITERS, 8, 128, 128), F32),
            pltpu.VMEM((8, 128, 128), F32),
            pltpu.VMEM((ITERS, 8, 128, 128), F32),
            pltpu.VMEM((ITERS, 7, 128, 128), F32),
            pltpu.VMEM((ITERS, 16, 2, 8, 128), F32),
            pltpu.VMEM((ITERS, 15, 2, 8, 128), F32),
            dma((3,)),
            dma((8,)),
            dma((8,)),
            dma,
            dma((10,)),
            dma((ITERS, 8)),
            dma((ITERS, 7)),
            dma((ITERS, 7)),
            dma((ITERS, 8)),
            dma((ITERS,)),
            dma((ITERS,)),
            dma,
            dma,
        ],
        compiler_params=pltpu.CompilerParams(
            collective_id=0, has_side_effects=True, vmem_limit_bytes=60 * 1024 * 1024
        ),
        name="glm_pca",
    )(
        counts.reshape(2, 2, 8, 128, 128),
        offsets.reshape(2, 2, 8, 128, 128),
        loadings.T,
        factors.T,
    )
    at_out, fac_out = pl.pallas_call(
        hand_over,
        out_shape=(
            jax.ShapeDtypeStruct((64, 4096), F32),
            jax.ShapeDtypeStruct((64, 128), F32),
        ),
        in_specs=[hbm_spec, hbm_spec],
        out_specs=(hbm_spec, hbm_spec),
        scratch_shapes=[pltpu.VMEM((64, 4096), F32), pltpu.VMEM((64, 128), F32), dma((5,)), dma((5,))],
        name="hand_over",
    )(at_out, fac_out)
    return at_out.T, fac_out.T


def solution(mesh):
    placed = (P("rows", "weeks"), P("rows", "weeks"), P("rows", None), P("weeks", None))
    return jax.shard_map(
        local,
        mesh=mesh,
        in_specs=placed,
        out_specs=(P("rows", None), P("weeks", None)),
        check_vma=False,
    )
```

```python
import functools

import jax
import jax.numpy as jnp
from jax import lax
from jax.experimental import pallas as pl
from jax.experimental.pallas import tpu as pltpu
from jax.sharding import PartitionSpec as P

ITERS = 2
F32 = jnp.float32
BF16 = jnp.bfloat16
MESH = pl.DeviceIdType.MESH
LATE = 3
LAG = 5
STAG = 1


def pack(digits):
    return sum(d * 8**i for i, d in enumerate(digits))


OWNERS = pack([4, 2, 6, 5, 3, 1, 7, 0])
TARGETS = pack([1, 1, 7, 5, 3, 1, 7])
OUTWARD = pack([0, 1, 7, 3, 5, 2, 6, 4])


def far_first(j):
    return 4 + (1 - 2 * lax.rem(j, 2)) * lax.div(j + 1, 2)


def split(v):
    hi = v.astype(BF16)
    lo = (v - hi.astype(F32)).astype(BF16)
    return hi, lo


def mm(a, b):
    return jnp.dot(a, b, preferred_element_type=F32)


def kernel(
    counts, offs, load, fac, at_out, fac_out,
    cnt, obf, off, osend, a0, xmat, weta, w1, w3, g1, g2,
    bt, at1, at2, xs, xr, so, zs, zr, gs, gr,
    s_loc, s_cnt, s_off, s_bt, s_send, s_x, s_z, s_agz, s_agx, s_g, s_b, s_sib, s_out,
):
    r = lax.axis_index("rows")
    w = lax.axis_index("weeks")
    z = lax.div(w, 4)
    xl = lax.rem(lax.div(w, 2), 2)
    c = lax.rem(w, 2)
    sib = (r, w + 1 - 2 * c)
    xp = (r, w + 2 - 4 * xl)
    own = xl * 8 + z

    def zdev(o):
        return (r, lax.rem(w + 4 * o, 32))

    def rdev(idx):
        return (lax.rem(idx, 8), w - c + lax.div(idx, 8))

    def zdst(seq):
        return lax.rem(z + lax.rem(seq, 8), 8)

    def zsrc(f):
        return lax.rem(z + 8 - far_first(f), 8)

    def remote(src, dst, ss, rs, dev):
        return pltpu.make_async_remote_copy(
            src_ref=src, dst_ref=dst, send_sem=ss, recv_sem=rs, device_id=dev, device_id_type=MESH
        )

    def wait_bytes(ref, sem):
        pltpu.make_async_copy(ref, ref, sem).wait()

    def put(h, b, carry):
        cols = pl.ds(pl.multiple_of((h * 16 + b) * 128, 128), 128)
        pltpu.make_async_copy(at2.at[h, b], at_out.at[:, cols], s_out).start()
        return carry

    me = c * 8 + r
    barrier = pltpu.get_barrier_semaphore()

    def greet_z(j, carry):
        pl.semaphore_signal(barrier, inc=1, device_id=zdev(j), device_id_type=MESH)
        return carry

    def greet_r(t, carry):
        pl.semaphore_signal(barrier, inc=1, device_id=rdev(lax.rem(me + t, 16)), device_id_type=MESH)
        return carry

    ld_off = pltpu.make_async_copy(offs, obf, s_loc.at[0])
    ld_cnt = pltpu.make_async_copy(counts.at[c], cnt.at[c], s_loc.at[1])
    ld_a0 = pltpu.make_async_copy(load.at[:, pl.ds(c * 2048, 2048)], a0, s_loc.at[2])
    ld_fac = pltpu.make_async_copy(fac, bt.at[0, c], s_loc.at[3])
    ld_off.start()
    ld_fac.start()
    ld_a0.start()
    ld_cnt.start()
    lax.fori_loop(1, 8, greet_z, 0)
    lax.fori_loop(1, 16, greet_r, 0)
    pl.semaphore_signal(barrier, inc=1, device_id=xp, device_id_type=MESH)


    def first(b):
        return a0[:, pl.ds(pl.multiple_of(b * 128, 128), 128)]

    def stack(hi, lo):
        return jnp.concatenate([hi.astype(F32), lo.astype(F32)], axis=0).T.astype(BF16)

    ld_off.wait()

    def widen(d, carry):
        for x in range(2):
            osend[x, d] = obf[1 - c, x, d].astype(F32)
            off[c, x, d] = obf[c, x, d].astype(F32)
        return carry

    lax.fori_loop(0, 8, widen, 0)
    ld_a0.wait()

    def first_x(b, carry):
        xmat[b] = stack(*split(first(b)))
        return carry

    lax.fori_loop(0, 16, first_x, 0)
    ld_cnt.wait()
    ld_fac.wait()
    pl.semaphore_wait(barrier, 23)

    remote(bt.at[0, c], bt.at[0, c], s_send.at[0], s_bt, sib).start()

    def swap(k, seq):
        d = zdst(seq)
        remote(counts.at[1 - c, :, d], cnt.at[c, :, d], s_send.at[1], s_cnt.at[k], sib).start()
        remote(osend.at[:, d], off.at[c, :, d], s_send.at[2], s_off.at[k], sib).start()
        return lax.div(seq, 8)

    lax.fori_loop(0, 8, swap, OWNERS)

    def week_weights(it):
        b = jnp.concatenate([bt[it, 0].reshape(64, 128), bt[it, 1].reshape(64, 128)], axis=1)
        bh, bl = split(b)
        qh, ql = split(b * b)
        weta[...] = jnp.concatenate([bh, bh, bl, bl], axis=0)
        bh, bl, qh, ql = (v.astype(F32) for v in (bh, bl, qh, ql))
        w1[...] = jnp.concatenate([bh, -qh, bl, -ql], axis=0).T.astype(BF16)
        zero = jnp.zeros_like(qh)
        w3[...] = jnp.concatenate([zero, qh, zero, ql], axis=0).T.astype(BF16)

    def residual(x, d):
        xb = xmat[x * 8 + d]
        eta = mm(jnp.concatenate([xb, xb], axis=1), weta[...])
        o = jnp.concatenate([off[0, x, d], off[1, x, d]], axis=1)
        n = jnp.concatenate([cnt[0, x, d], cnt[1, x, d]], axis=1).astype(F32)
        res = n - jnp.exp(eta + o)
        rh, rl = split(res)
        return rh, rl, n.astype(BF16)

    def left(x, d):
        rh, rl, n = residual(x, d)
        o = mm(rh, w1[...]) + mm(n, w3[...])
        return o[:, :128] + o[:, 128:] + mm(rl, w1[:, :128])

    def right(at, x, d):
        a = at[x * 8 + d]
        hi, lo = split(a)
        ph, pw = split(a * a)
        xmat[x * 8 + d] = stack(hi, lo)
        rh, rl, n = residual(x, d)
        lt = jnp.concatenate([hi, -ph, lo, -pw], axis=0)
        g1[...] += mm(lt, rh)
        g2[:128] += mm(lt[:128], rl)
        g2[128:] += mm(jnp.concatenate([ph, pw], axis=0), n)

    for it in range(ITERS):
        last = it == ITERS - 1
        at = at2.at[c] if last else at1
        if it == 0:
            pltpu.make_async_copy(bt.at[0, 1 - c], bt.at[0, 1 - c], s_bt).wait()
        week_weights(it)

        def finish(it=it, at=at):
            def z_sum(f, total):
                wait_bytes(zr.at[it, f], s_z.at[it, f])
                return total + zr[it, f]

            total = lax.fori_loop(3, 7, z_sum, zs[it, 7]).T
            old = first(own) if it == 0 else at1[own]
            at[own] = old + total[:64] / (1.0 + total[64:])

            def ag_send(p, seq):
                remote(
                    at.at[own], at.at[own], s_send.at[6], s_agz.at[it, p], zdev(lax.rem(seq, 8))
                ).start()
                return lax.div(seq, 8)

            lax.fori_loop(0, 4, ag_send, OUTWARD // 8)
            remote(at.at[own], at.at[own], s_send.at[5], s_agx.at[it, 7], xp).start()

        def emit(j, d, x, it=it):
            v = left(x, d)

            @pl.when(x == xl)
            def _():
                so[j] = v

            @pl.when(x != xl)
            def _():
                xs[it, j] = v
                remote(xs.at[it, j], xr.at[it, j], s_send.at[3], s_x.at[it, j], xp).start()

        def a_one(j, seq, it=it, emit=emit):
            d = zdst(seq)
            if it == 0:
                wait_bytes(cnt.at[1 - c, :, d], s_cnt.at[j])
                wait_bytes(off.at[1 - c, :, d], s_off.at[j])
            emit(j, d, lax.rem(xl + 1 + c * STAG, 2))
            return lax.div(seq, 8)

        def a_two(j, carry, it=it, emit=emit):
            seq, target = carry

            @pl.when(j < 8)
            def _():
                emit(j, zdst(seq), lax.rem(xl + c * STAG, 2))

            f = j - LATE * c * STAG

            @pl.when((f >= 0) & (f < 8))
            def _():
                wait_bytes(xr.at[it, f], s_x.at[it, f])
                zs[it, f] = so[f] + xr[it, f]

                @pl.when((f >= 4) & (f < 7))
                def _():
                    wait_bytes(zr.at[it, f - 4], s_z.at[it, f - 4])
                    zs[it, f] += zr[it, f - 4]

                @pl.when(f < 7)
                def _():
                    remote(
                        zs.at[it, f], zr.at[it, f], s_send.at[4], s_z.at[it, f], zdev(lax.rem(target, 8))
                    ).start()

            return lax.div(seq, 8), lax.div(target, 8)

        lax.fori_loop(0, 8, a_one, OWNERS)
        delayed = TARGETS * (1 + c * STAG * (8**LATE - 1))
        lax.fori_loop(0, 8 + LATE * STAG, a_two, (jnp.int32(OWNERS), delayed))
        finish()

        g1[...] = jnp.zeros_like(g1)
        g2[...] = jnp.zeros_like(g2)

        def b_step(k, carry, it=it, at=at):
            seq, late = carry

            @pl.when(k < 8)
            def _():
                d = lax.rem(z + 8 - lax.rem(seq, 8), 8)

                @pl.when(k > 0)
                def _():
                    p = k - 1
                    blk = at.at[xl * 8 + d]
                    wait_bytes(blk, s_agz.at[it, p])

                    @pl.when(p < 3)
                    def _():
                        on = 1 + 6 * lax.rem(p, 2)
                        remote(blk, blk, s_send.at[6], s_agz.at[it, p + 4], zdev(on)).start()

                    remote(blk, blk, s_send.at[5], s_agx.at[it, p], xp).start()

                right(at, xl, d)

            @pl.when(k >= LAG)
            def _():
                d = lax.rem(z + 8 - lax.rem(late, 8), 8)
                wait_bytes(at.at[(1 - xl) * 8 + d], s_agx.at[it, lax.rem(k + 7 - LAG, 8)])
                right(at, 1 - xl, d)

            return lax.div(seq, 8), lax.select(k >= LAG, lax.div(late, 8), late)

        lax.fori_loop(0, 8 + LAG, b_step, (jnp.int32(OUTWARD), jnp.int32(OUTWARD)))

        if last:
            remote(at2.at[c], at2.at[c], s_send.at[7], s_sib, sib).start()
            lax.fori_loop(0, 16, functools.partial(put, c), 0)

        grad = g1[0:64] + g1[128:192] + g2[0:64]
        curv = g1[64:128] + g1[192:256] + g2[64:128] + g2[128:192] + g2[192:256]
        for h in range(2):
            for o in range(8):
                gs[it, h * 8 + o, 0] = grad[8 * o : 8 * o + 8, 128 * h : 128 * h + 128]
                gs[it, h * 8 + o, 1] = curv[8 * o : 8 * o + 8, 128 * h : 128 * h + 128]

        def g_send(t, carry, it=it):
            u = 1 + lax.rem(t + 3, 15)
            idx = lax.rem(me + u, 16)
            remote(gs.at[it, idx], gr.at[it, u - 1], s_send.at[8], s_g.at[it], rdev(idx)).start()
            return carry

        lax.fori_loop(1, 16, g_send, 0)
        wait_bytes(gr.at[it], s_g.at[it])
        tot = gs[it, me]
        for t in range(15):
            tot = tot + gr[it, t]
        bt[it + 1, c, r] = bt[it, c, r] + tot[0] / (1.0 + tot[1])
        mine = bt.at[it + 1, c, r]

        if last:
            def b_send(t, carry, mine=mine, it=it):
                dev = (lax.rem(r + t, 8), w)
                remote(mine, mine, s_send.at[9], s_b.at[it], dev).start()
                return carry

            lax.fori_loop(1, 8, b_send, 0)
            wait_bytes(gr.at[it, pl.ds(0, 7), 0], s_b.at[it])
        else:
            def b_send(t, carry, mine=mine, it=it):
                remote(mine, mine, s_send.at[9], s_b.at[it], rdev(lax.rem(me + 1 + lax.rem(t + 3, 15), 16))).start()
                return carry

            lax.fori_loop(1, 16, b_send, 0)
            wait_bytes(gr.at[it, :, 0], s_b.at[it])

    fac_out[...] = bt[ITERS, c].reshape(64, 128)
    wait_bytes(at2.at[1 - c], s_sib)
    lax.fori_loop(0, 16, functools.partial(put, 1 - c), 0)

    wait_bytes(bt.at[0, c], s_send.at[0])
    wait_bytes(cnt.at[c], s_send.at[1])
    wait_bytes(osend, s_send.at[2])
    wait_bytes(xs, s_send.at[3])
    wait_bytes(zs.at[:, pl.ds(0, 7)], s_send.at[4])
    wait_bytes(at1, s_send.at[5])
    wait_bytes(at1.at[pl.ds(0, 14)], s_send.at[6])
    wait_bytes(at2.at[c], s_send.at[7])
    wait_bytes(gr, s_send.at[8])
    wait_bytes(gr.at[0, :, 0], s_send.at[9])
    wait_bytes(gr.at[0, pl.ds(0, 7), 0], s_send.at[9])
    wait_bytes(at2, s_out)


def hand_over(a_ref, f_ref, a_out, f_out, sem):
    moves = [pltpu.make_async_copy(f_ref, f_out, sem.at[4])]
    for i in range(4):
        rows = pl.ds(16 * i, 16)
        moves.append(pltpu.make_async_copy(a_ref.at[rows], a_out.at[rows], sem.at[i]))
    for move in moves:
        move.start()
    for move in moves:
        move.wait()


def local(counts, offsets, loadings, factors):
    any_spec = pl.BlockSpec(memory_space=pl.ANY)
    hbm_spec = pl.BlockSpec(memory_space=pltpu.HBM)
    vmem_spec = pl.BlockSpec(memory_space=pltpu.VMEM)
    dma = pltpu.SemaphoreType.DMA
    at_out, fac_out = pl.pallas_call(
        kernel,
        out_shape=(
            jax.ShapeDtypeStruct((64, 4096), F32),
            jax.ShapeDtypeStruct((64, 128), F32),
        ),
        in_specs=[any_spec, any_spec, any_spec, hbm_spec],
        out_specs=(any_spec, vmem_spec),
        scratch_shapes=[
            pltpu.VMEM((2, 2, 8, 128, 128), jnp.int32),
            pltpu.VMEM((2, 2, 8, 128, 128), BF16),
            pltpu.VMEM((2, 2, 8, 128, 128), F32),
            pltpu.VMEM((2, 8, 128, 128), F32),
            pltpu.VMEM((64, 2048), F32),
            pltpu.VMEM((16, 128, 128), BF16),
            pltpu.VMEM((256, 256), BF16),
            pltpu.VMEM((256, 256), BF16),
            pltpu.VMEM((256, 256), BF16),
            pltpu.VMEM((256, 256), F32),
            pltpu.VMEM((256, 256), F32),
            pltpu.VMEM((ITERS + 1, 2, 8, 8, 128), F32),
            pltpu.VMEM((16, 64, 128), F32),
            pltpu.VMEM((2, 16, 64, 128), F32),
            pltpu.VMEM((ITERS, 8, 128, 128), F32),
            pltpu.VMEM((ITERS, 8, 128, 128), F32),
            pltpu.VMEM((8, 128, 128), F32),
            pltpu.VMEM((ITERS, 8, 128, 128), F32),
            pltpu.VMEM((ITERS, 7, 128, 128), F32),
            pltpu.VMEM((ITERS, 16, 2, 8, 128), F32),
            pltpu.VMEM((ITERS, 15, 2, 8, 128), F32),
            dma((4,)),
            dma((8,)),
            dma((8,)),
            dma,
            dma((10,)),
            dma((ITERS, 8)),
            dma((ITERS, 7)),
            dma((ITERS, 7)),
            dma((ITERS, 8)),
            dma((ITERS,)),
            dma((ITERS,)),
            dma,
            dma,
        ],
        compiler_params=pltpu.CompilerParams(
            collective_id=0, has_side_effects=True, vmem_limit_bytes=52 * 1024 * 1024
        ),
        name="glm_pca",
    )(
        counts.reshape(2, 2, 8, 128, 128),
        offsets.reshape(2, 2, 8, 128, 128),
        loadings.T,
        factors.T.reshape(8, 8, 128),
    )
    at_out, fac_out = pl.pallas_call(
        hand_over,
        out_shape=(
            jax.ShapeDtypeStruct((64, 4096), F32),
            jax.ShapeDtypeStruct((64, 128), F32),
        ),
        in_specs=[any_spec, any_spec],
        out_specs=(hbm_spec, hbm_spec),
        scratch_shapes=[dma((5,))],
        compiler_params=pltpu.CompilerParams(vmem_limit_bytes=1024 * 1024),
        name="hand_over",
    )(at_out, fac_out)
    return at_out.T, fac_out.T


def solution(mesh):
    placed = (P("rows", "weeks"), P("rows", "weeks"), P("rows", None), P("weeks", None))
    return jax.shard_map(
        local,
        mesh=mesh,
        in_specs=placed,
        out_specs=(P("rows", None), P("weeks", None)),
        check_vma=False,
    )
```
